256 devices in a mesh: segment: 8 (over y, core), ctx: 32 (over z, x).
Axes of the slice: x: 4, y: 4, z: 8, core: 2. Of those that a mesh axis runs over, the one named last changes fastest.
Arguments:
- queries: bfloat16 [256, 8192], P(('segment', 'ctx')), may hold values from -9 to 9
- cache: bfloat16 [524288, 2048], P(('segment', 'ctx')), may hold values from -9 to 9
- out_weight: bfloat16 [65536, 8192], P('segment', 'ctx'), may hold values from -2 to 2
- offsets: int32 [8], P('segment'), may hold values from 21845 to 65504, as said below
- starts: int32 [8], P('segment'), may hold values from 0 to 37422, as said below
Outputs:
- advanced: bfloat16 [256, 8192], P('segment', 'ctx')
The draws below stay inside these ranges and needn't reach their ends.
Inputs may be any that keep to these rules, and one draw needn't show every extreme that they name: `offsets`: each section's slice ends inside its cache; some section's slice ends at its last cache position. A section's document starts no later than its first query; some section's document starts at 0.
All inputs are finite; a program needn't handle non-finite values.
Results may differ from the reference program's by a relative error of at most 0.0054.
Values may be sent and summed in bfloat16 or wider, within the bound.
A program may use at most 192 MiB of HBM per device.

```python
import jax
import jax.numpy as jnp
from jax import lax

D = 8192
H = 64
KVH = 8
HD = 128
QS = 32
CD = 2048
SECTIONS = 8
LMAX = 65536
N_CTX = 32


def section_plan(key):
    order = jax.random.permutation(jax.random.fold_in(key, 101), SECTIONS).astype(jnp.int32)
    lowest = LMAX // 3
    highest = LMAX - QS
    span = lowest + (highest - lowest) * order // max(SECTIONS - 1, 1)
    drawn = jax.random.randint(jax.random.fold_in(key, 102), (SECTIONS,), 0, highest - span + 1)
    doc_start = jnp.where(order == 0, 0, jnp.where(order == 1, highest - span, drawn))
    return ((doc_start + span).astype(jnp.int32), doc_start.astype(jnp.int32))


def draw_offsets(key, part):
    return section_plan(key)[0]


def draw_starts(key, part):
    return section_plan(key)[1]


def draw_queries(key, part):
    values = jax.random.normal(jax.random.fold_in(key, 1), (SECTIONS * QS, H * HD), jnp.float32)
    values = values * 1.5
    return jnp.clip(values, -9.0, 9.0).astype(jnp.bfloat16)


def draw_cache(key, part):
    values = jnp.clip(jax.random.normal(jax.random.fold_in(key, 5), (SECTIONS * LMAX, 2 * KVH * HD), jnp.float32), -5.0, 5.0)
    return jnp.clip(values, -9.0, 9.0).astype(jnp.bfloat16)


def steps_of(own_key, dims, shards, low, high):
    def one(position, parts):
        draws = jax.random.uniform(jax.random.fold_in(jax.random.fold_in(own_key, 6), position), (parts,), jnp.float32, low / len(shards), high / len(shards))
        return jnp.repeat(jnp.exp(draws), dims[position] // parts).reshape((-1,) + (1,) * (len(dims) - position - 1))

    gain = one(*shards[0])
    for cut in shards[1:]:
        gain = gain * one(*cut)
    return gain


def centred(key, shape, spread, bound, cuts=(), held_as=jnp.bfloat16):
    entries = jax.random.normal(key, shape, jnp.float32) * spread
    if len(cuts) > 0:
        entries = steps_of(key, shape, cuts, -0.22, 0.18) * entries
    return jnp.clip(entries, min=-bound, max=bound).astype(held_as)


def setup_inputs(seed: int = 0) -> dict:
    key_list = jax.random.split(jax.random.key(seed), 6)
    return {
        "queries": draw_queries(jax.random.fold_in(key_list[5], 71), 0),
        "cache": draw_cache(jax.random.fold_in(key_list[5], 71), 0),
        "out_weight": centred(key_list[2], (SECTIONS * H * HD, D), (max(H * HD // 1024, 1)) ** -0.5, 2.0, ((0, 8), (1, 32))),
        "offsets": draw_offsets(jax.random.fold_in(key_list[5], 71), 0),
        "starts": draw_starts(jax.random.fold_in(key_list[5], 71), 0),
    }


def block_state(query_block, cache_block, offset, doc_start, first_position):
    rows = query_block.shape[0]
    span = cache_block.shape[0]
    positions = first_position + jnp.arange(span, dtype=jnp.int32)
    query_pos = offset + jnp.arange(rows, dtype=jnp.int32)
    visible = (positions[None, :] >= doc_start) & (positions[None, :] <= query_pos[:, None])
    visible = visible[:, None, None, :]
    keys = cache_block[:, :KVH * HD].reshape(span, KVH, HD).astype(jnp.float32)
    values = cache_block[:, KVH * HD:].reshape(span, KVH, HD).astype(jnp.float32)
    scores = jnp.einsum('qgjd,pgd->qgjp', query_block, keys) * (HD ** -0.5)
    masked = jnp.where(visible, scores, -1e30)
    row_max = jnp.max(masked, axis=-1)
    weights = jnp.where(visible, jnp.exp(masked - row_max[..., None]), 0.0)
    weight_sum = jnp.sum(weights, axis=-1)
    rounded = lax.optimization_barrier(weights.astype(jnp.bfloat16)).astype(jnp.float32)
    numerator = jnp.einsum('qgjp,pgd->qgjd', rounded, values)
    outputs = numerator / jnp.maximum(weight_sum, 1.0)[..., None]
    return row_max, weight_sum, outputs


def reference(queries, cache, out_weight, offsets, starts):
    results = []
    tile = CD // 2
    for section in range(SECTIONS):
        query_block = queries[section * QS:(section + 1) * QS].reshape(QS, KVH, H // KVH, HD).astype(jnp.float32)
        section_cache = cache[section * LMAX:(section + 1) * LMAX]
        offset = offsets[section]
        doc_start = starts[section]

        def one_tile(index):
            block = lax.dynamic_slice_in_dim(section_cache, index * tile, tile, 0)
            return block_state(query_block, block, offset, doc_start, index * tile)

        maxima, sums, outputs = lax.map(one_tile, jnp.arange(2 * N_CTX, dtype=jnp.int32))
        overall = jnp.max(maxima, axis=0)
        factors = sums * jnp.exp(maxima - overall[None])
        attention = jnp.sum(factors[..., None] * outputs, axis=0) / jnp.sum(factors, axis=0)[..., None]
        attention = attention.reshape(QS, H * HD).astype(jnp.bfloat16)
        weight_rows = out_weight[section * H * HD:(section + 1) * H * HD]
        projected = jnp.dot(attention, weight_rows, preferred_element_type=jnp.float32).astype(jnp.bfloat16)
        results.append(projected)
    return jnp.concatenate([results[-1]] + results[:-1], axis=0)
```

```python
import functools

import jax
import jax.numpy as jnp
from jax import lax
from jax.experimental import pallas as pl
from jax.experimental.pallas import tpu as pltpu
from jax.sharding import PartitionSpec as P

H = 64
KVH = 8
HD = 128
GROUP = H // KVH
NX = 4
NZ = 8
QS = NX * NZ
ROWS = QS * GROUP
CHUNK = ROWS // NX
SCALE2 = HD ** (-0.5) * 1.4426950408889634
HIDDEN = -1e30
MESH = pl.DeviceIdType.MESH
FAR_FIRST = (4, 3, -3, 2, -2, 1, -1, 0)


def kernel(offsets, starts, q_hbm, cache_hbm, w_hbm, out_ref, qrow, qf, qbuf, qg, fbuf, kbuf, vbuf,
           wbuf, sbuf, pbuf, osend, ostat, xbuf, xstat, zsend, zsstat, zbuf, zstat, abuf, ysend,
           q_load, k_load, v_load, w_load, qz_s, qz_r, qx_s, qx_r, xs_s, xs_r, zs_s, zs_r, az_s,
           az_r, ax_s, ax_r, y_s, y_r):
    segment = lax.axis_index("segment")
    ctx = lax.axis_index("ctx")
    z = ctx // NX
    x = ctx % NX
    n_seg = lax.axis_size("segment")
    span = cache_hbm.shape[0]

    def at_z(step):
        return (z + step + NZ) % NZ

    def at_x(step):
        return (x + step + NX) % NX

    def peer(zz, xx):
        return {"segment": segment, "ctx": zz * NX + xx}

    barrier = pltpu.get_barrier_semaphore()
    for step in range(1, NZ):
        pl.semaphore_signal(barrier, inc=1, device_id=peer(at_z(step), x), device_id_type=MESH)
    for step in range(1, NX):
        pl.semaphore_signal(barrier, inc=1, device_id=peer(z, at_x(step)), device_id_type=MESH)
    before = (segment + n_seg - 1) % n_seg
    after = (segment + 1) % n_seg
    pl.semaphore_signal(
        barrier, inc=1, device_id={"segment": before, "ctx": ctx}, device_id_type=MESH
    )

    q_copy = pltpu.make_async_copy(q_hbm, qrow, q_load)
    q_copy.start()
    k_copies, v_copies = [], []
    for k, dz in enumerate(FAR_FIRST):
        g = at_z(dz)
        k_copies.append(pltpu.make_async_copy(
            cache_hbm.at[:, pl.ds(pl.multiple_of(g * HD, HD), HD)], kbuf.at[k], k_load.at[k]))
        v_copies.append(pltpu.make_async_copy(
            cache_hbm.at[:, pl.ds(pl.multiple_of((KVH + g) * HD, HD), HD)], vbuf.at[k], v_load.at[k]))
        k_copies[k].start()
        v_copies[k].start()
    w_copy = pltpu.make_async_copy(w_hbm, wbuf, w_load)
    w_copy.start()

    q_copy.wait()
    row = qrow[...].astype(jnp.float32)
    for h in range(H):
        qf[h:h + 1, :] = row[:, h * HD:(h + 1) * HD]
    qbuf[ctx] = qf[...].astype(jnp.bfloat16)

    pl.semaphore_wait(barrier, NZ - 1 + NX - 1 + 1)

    def gather(buf, z_send, z_recv, x_send, x_recv, use):
        def along_z(i):
            return pltpu.make_async_remote_copy(
                buf.at[ctx], buf.at[ctx], z_send.at[i], z_recv.at[i],
                device_id=peer(at_z(FAR_FIRST[i]), x), device_id_type=MESH)

        def along_x(i, dx):
            own = at_z(-FAR_FIRST[i]) * NX + x
            return pltpu.make_async_remote_copy(
                buf.at[own], buf.at[own], x_send.at[i, dx - 1], x_recv.at[i, dx - 1],
                device_id=peer(z, at_x(dx)), device_id_type=MESH)

        for i in range(NZ - 1):
            along_z(i).start()
        for dx in range(1, NX):
            along_x(NZ - 1, dx).start()
        use(ctx)
        for i in reversed(range(NZ - 1)):
            along_z(i).wait_recv()
            for dx in range(1, NX):
                along_x(i, dx).start()
            use(at_z(-FAR_FIRST[i]) * NX + x)
        for i in reversed(range(NZ)):
            for dx in range(1, NX):
                along_x(i, dx).wait_recv()
                use(at_z(-FAR_FIRST[i]) * NX + at_x(-dx))

        def finish():
            for i in range(NZ - 1):
                along_z(i).wait_send()
            for i in range(NZ):
                for dx in range(1, NX):
                    along_x(i, dx).wait_send()
        return finish

    offset = offsets[0]
    start = starts[0]
    first = ctx * span
    lanes = lax.broadcasted_iota(jnp.int32, (span // 8, HD), 1)
    for part in range(8):
        position = first + part * (span // 8) + lax.broadcasted_iota(jnp.int32, (span // 8, HD), 0)
        late = jnp.clip(position - offset, 0, QS)
        late = jnp.where(position < start, QS, late)
        fbuf[part * (span // 8):(part + 1) * (span // 8), :] = jnp.where(
            late == lanes, 1.0, 0.0).astype(jnp.bfloat16)
    g_lane = lax.broadcasted_iota(jnp.int32, (ROWS, HD), 1)
    g_row = lax.broadcasted_iota(jnp.int32, (ROWS, HD), 0) % QS
    hide = jnp.where((g_lane > g_row) & (g_lane <= QS), HIDDEN, 0.0).astype(jnp.bfloat16)

    def use_query(c):
        value = qbuf[c].astype(jnp.float32)
        for g in range(KVH):
            qg[g, pl.ds(c, GROUP, stride=QS), :] = value[g * GROUP:(g + 1) * GROUP, :]

    finish_q = gather(qbuf, qz_s, qz_r, qx_s, qx_r, use_query)

    lane = lax.broadcasted_iota(jnp.int32, (CHUNK, HD), 1)
    line = lax.broadcasted_iota(jnp.int32, (CHUNK, HD), 0)
    diagonal = lane == line
    diagonal_high = lane == line + CHUNK
    low = lax.broadcasted_iota(jnp.int32, (1, HD), 1) < CHUNK

    def x_copies(k, dx):
        to = at_x(dx)
        where = peer(z, to)
        return (
            pltpu.make_async_remote_copy(
                osend.at[k, pl.ds(pl.multiple_of(to * CHUNK, CHUNK), CHUNK), :],
                xbuf.at[k, dx - 1], xs_s.at[k, dx - 1, 0], xs_r.at[k, dx - 1, 0],
                device_id=where, device_id_type=MESH),
            pltpu.make_async_remote_copy(
                ostat.at[k, to, pl.ds(0, 1), :], xstat.at[k, dx - 1, pl.ds(0, 1), :],
                xs_s.at[k, dx - 1, 1], xs_r.at[k, dx - 1, 1],
                device_id=where, device_id_type=MESH),
        )

    def z_copies(k, dz):
        where = peer(at_z(dz), x)
        return (
            pltpu.make_async_remote_copy(
                zsend.at[k], zbuf.at[k], zs_s.at[k, 0], zs_r.at[k, 0],
                device_id=where, device_id_type=MESH),
            pltpu.make_async_remote_copy(
                zsstat.at[k, pl.ds(0, 1), :], zstat.at[k, pl.ds(0, 1), :],
                zs_s.at[k, 1], zs_r.at[k, 1], device_id=where, device_id_type=MESH),
        )

    def attend(k, carry):
        pltpu.make_async_copy(
            cache_hbm.at[:, pl.ds(0, HD)], kbuf.at[k], k_load.at[k]).wait()
        pltpu.make_async_copy(
            cache_hbm.at[:, pl.ds(0, HD)], vbuf.at[k], v_load.at[k]).wait()
        magnitude = NZ // 2 - (k + 1) // 2
        g = at_z((2 * (k % 2) - 1) * magnitude)
        query = jnp.concatenate([qg[g].astype(jnp.bfloat16), hide], axis=1)
        tile = 256
        for c in range(span // tile):
            rows = slice(c * tile, (c + 1) * tile)
            keys = jnp.concatenate([kbuf[k, rows, :], fbuf[rows, :]], axis=1)
            sbuf[:, rows] = lax.dot_general(
                query, keys, (((1,), (1,)), ((), ())), preferred_element_type=jnp.float32)
        block = 16
        maxima, sums = [], []
        for r in range(ROWS // block):
            rows = slice(r * block, (r + 1) * block)
            score = sbuf[rows, :]
            top = jnp.max(score, axis=1, keepdims=True)
            weight = jnp.exp2((score - top) * SCALE2)
            maxima.append(jnp.broadcast_to(top * SCALE2, (block, HD)))
            sums.append(jnp.broadcast_to(jnp.sum(weight, axis=1, keepdims=True), (block, HD)))
            pbuf[rows, :] = weight.astype(jnp.bfloat16)
        per = CHUNK // block
        for xx in range(NX):
            top = jnp.concatenate(maxima[xx * per:(xx + 1) * per], axis=0)
            total = jnp.concatenate(sums[xx * per:(xx + 1) * per], axis=0)
            stat = jnp.where(diagonal, top, 0.0) + jnp.where(diagonal_high, total, 0.0)
            ostat[k, xx, 0:1, :] = jnp.sum(stat, axis=0, keepdims=True)
        numerator = jnp.dot(pbuf[...], vbuf[k], preferred_element_type=jnp.float32)
        osend[k] = numerator.astype(jnp.bfloat16)
        for dx in range(1, NX):
            for copy in x_copies(k, dx):
                copy.start()
        return carry

    lax.fori_loop(0, KVH, attend, 0)

    def join(parts):
        stats = [stat for stat, _ in parts]
        top = functools.reduce(jnp.maximum, stats)
        total = jnp.zeros_like(top)
        mixed = jnp.zeros((CHUNK, HD), jnp.float32)
        for stat, numerator in parts:
            factor = jnp.exp2(stat - top)
            total = total + pltpu.roll(factor, CHUNK, 1) * stat
            column = jnp.sum(
                jnp.where(diagonal, jnp.broadcast_to(factor, (CHUNK, HD)), 0.0),
                axis=1, keepdims=True)
            mixed = mixed + column * numerator.astype(jnp.float32)
        return jnp.where(low, top, total), mixed

    own_rows = pl.ds(pl.multiple_of(x * CHUNK, CHUNK), CHUNK)
    for k, dz in enumerate(FAR_FIRST):
        parts = [(ostat[k, x, 0:1, :], osend[k, own_rows, :])]
        for dx in range(1, NX):
            for copy in x_copies(k, dx):
                copy.wait_recv()
            parts.append((xstat[k, dx - 1, 0:1, :], xbuf[k, dx - 1]))
        stat, mixed = join(parts)
        zsend[k] = mixed.astype(jnp.bfloat16)
        zsstat[k, 0:1, :] = stat
        if dz != 0:
            for copy in z_copies(k, dz):
                copy.start()

    own = NZ - 1
    parts = [(zsstat[own, 0:1, :], zsend[own])]
    for k in reversed(range(NZ - 1)):
        for copy in z_copies(k, FAR_FIRST[k]):
            copy.wait_recv()
        parts.append((zstat[k, 0:1, :], zbuf[k]))
    stat, mixed = join(parts)
    divisor = jnp.sum(
        jnp.where(diagonal_high, jnp.broadcast_to(stat, (CHUNK, HD)), 0.0), axis=1, keepdims=True)
    mixed = mixed / divisor
    abuf[ctx] = jnp.concatenate([mixed[:QS], mixed[QS:]], axis=1).astype(jnp.bfloat16)

    w_copy.wait()
    projected = [jnp.zeros((QS, out_ref.shape[1]), jnp.float32)]

    def use_chunk(c):
        projected[0] = projected[0] + jnp.dot(
            abuf[c], wbuf[pl.ds(pl.multiple_of(c * 2 * HD, 2 * HD), 2 * HD), :],
            preferred_element_type=jnp.float32)

    finish_a = gather(abuf, az_s, az_r, ax_s, ax_r, use_chunk)
    ysend[...] = projected[0].astype(jnp.bfloat16)
    y_copy = pltpu.make_async_remote_copy(
        ysend, out_ref, y_s.at[0], y_r.at[0],
        device_id={"segment": after, "ctx": ctx}, device_id_type=MESH)
    y_copy.start()
    finish_q()
    finish_a()
    for k, dz in enumerate(FAR_FIRST):
        for dx in range(1, NX):
            for copy in x_copies(k, dx):
                copy.wait_send()
        if dz != 0:
            for copy in z_copies(k, dz):
                copy.wait_send()
    y_copy.wait()


def per_device(queries, cache, out_weight, offsets, starts):
    span = cache.shape[0]
    columns = out_weight.shape[1]
    bf16, f32 = jnp.bfloat16, jnp.float32
    dma = pltpu.SemaphoreType.DMA
    return pl.pallas_call(
        kernel,
        out_shape=jax.ShapeDtypeStruct((QS, columns), bf16),
        in_specs=[pl.BlockSpec(memory_space=pltpu.SMEM)] * 2 + [pl.BlockSpec(memory_space=pl.ANY)] * 3,
        out_specs=pl.BlockSpec(memory_space=pltpu.VMEM),
        scratch_shapes=[
            pltpu.VMEM((1, H * HD), bf16),
            pltpu.VMEM((H, HD), f32),
            pltpu.VMEM((QS, H, HD), bf16),
            pltpu.VMEM((KVH, ROWS, HD), f32),
            pltpu.VMEM((span, HD), bf16),
            pltpu.VMEM((KVH, span, HD), bf16),
            pltpu.VMEM((KVH, span, HD), bf16),
            pltpu.VMEM((H * HD, columns), bf16),
            pltpu.VMEM((ROWS, span), f32),
            pltpu.VMEM((ROWS, span), bf16),
            pltpu.VMEM((KVH, ROWS, HD), bf16),
            pltpu.VMEM((KVH, NX, 8, HD), f32),
            pltpu.VMEM((KVH, NX - 1, CHUNK, HD), bf16),
            pltpu.VMEM((KVH, NX - 1, 8, HD), f32),
            pltpu.VMEM((NZ, CHUNK, HD), bf16),
            pltpu.VMEM((NZ, 8, HD), f32),
            pltpu.VMEM((NZ, CHUNK, HD), bf16),
            pltpu.VMEM((NZ, 8, HD), f32),
            pltpu.VMEM((QS, QS, 2 * HD), bf16),
            pltpu.VMEM((QS, columns), bf16),
            dma, dma((KVH,)), dma((KVH,)), dma,
            dma((NZ - 1,)), dma((NZ - 1,)), dma((NZ, NX - 1)), dma((NZ, NX - 1)),
            dma((KVH, NX - 1, 2)), dma((KVH, NX - 1, 2)),
            dma((NZ - 1, 2)), dma((NZ - 1, 2)),
            dma((NZ - 1,)), dma((NZ - 1,)), dma((NZ, NX - 1)), dma((NZ, NX - 1)),
            dma((1,)), dma((1,)),
        ],
        compiler_params=pltpu.CompilerParams(collective_id=0, has_side_effects=True),
        name="section_attention",
    )(offsets, starts, queries, cache, out_weight)


def solution(mesh):
    in_specs = (
        P(("segment", "ctx"), None),
        P(("segment", "ctx"), None),
        P("segment", "ctx"),
        P("segment"),
        P("segment"),
    )
    out_specs = P("segment", "ctx")
    return jax.shard_map(
        per_device, mesh=mesh, in_specs=in_specs, out_specs=out_specs, check_vma=False
    )
```

```python
import functools

import jax
import jax.numpy as jnp
from jax import lax
from jax.experimental import pallas as pl
from jax.experimental.pallas import tpu as pltpu
from jax.sharding import PartitionSpec as P

VMEM_LIMIT = 40 * 1024 * 1024
H = 64
KVH = 8
HD = 128
GROUP = H // KVH
NX = 4
NZ = 8
QS = NX * NZ
ROWS = QS * GROUP
CHUNK = ROWS // NX
SCALE2 = HD ** (-0.5) * 1.4426950408889634
HIDDEN = -1e30
MESH = pl.DeviceIdType.MESH
FAR_FIRST = (4, 3, -3, 2, -2, 1, -1, 0)
Z_NEAR = (6, 5)
Z_FAR = (4, 3, 2, 1, 0)
FIRST_AT, FIRST_N, FIRST_HEADS = 3, 2, (1, 0)
REST_AT, REST_N, REST_HEADS = 5, 6, (2, 4, 6, 7, 5, 3)
SEND_AFTER = {3: (0, 1), 5: (2, 3), 7: (4, 5), 8: (6,), 9: (7,)}
JOIN_AFTER = {8: (0,), 9: (1, 2, 3, 4, 5, 6, 7)}


def kernel(off_hbm, start_hbm, q_hbm, cache_hbm, w_hbm, out_ref, off_smem, start_smem, qrow, qf,
           qdup, first_q, rest_q, qg, qb, hide, fbuf, kbuf, vbuf, wbuf, s_even, s_odd, p_even,
           p_odd, partial, osend, ostat, xbuf, xstat, zsend, zsstat, zbuf, zstat, abuf, ysend, small_load,
           q_load, k_load, v_load, w_load, fz_s, fz_r, fx_s, fx_r, rz_s, rz_r, rx_s, rx_r, xs_s,
           xs_r, zs_s, zs_r, az_s, az_r, ax_s, ax_r, y_s, y_r):
    segment = lax.axis_index("segment")
    ctx = lax.axis_index("ctx")
    z = ctx // NX
    x = ctx % NX
    n_seg = lax.axis_size("segment")
    span = cache_hbm.shape[0]
    bf16, f32 = jnp.bfloat16, jnp.float32

    def at_z(step):
        return (z + step + NZ) % NZ

    def at_x(step):
        return (x + step + NX) % NX

    def peer(zz, xx):
        return {"segment": segment, "ctx": zz * NX + xx}

    barrier = pltpu.get_barrier_semaphore()
    for step in range(1, NZ):
        pl.semaphore_signal(barrier, inc=1, device_id=peer(at_z(step), x), device_id_type=MESH)
    for step in range(1, NX):
        pl.semaphore_signal(barrier, inc=1, device_id=peer(z, at_x(step)), device_id_type=MESH)
    before = (segment + n_seg - 1) % n_seg
    after = (segment + 1) % n_seg
    pl.semaphore_signal(
        barrier, inc=1, device_id={"segment": before, "ctx": ctx}, device_id_type=MESH
    )

    q_copy = pltpu.make_async_copy(q_hbm, qrow, q_load)
    q_copy.start()
    off_copy = pltpu.make_async_copy(off_hbm, off_smem, small_load.at[0])
    start_copy = pltpu.make_async_copy(start_hbm, start_smem, small_load.at[1])
    off_copy.start()
    start_copy.start()
    k_copies, v_copies = [], []
    for k, dz in enumerate(FAR_FIRST):
        g = at_z(dz)
        k_copies.append(pltpu.make_async_copy(
            cache_hbm.at[:, pl.ds(pl.multiple_of(g * HD, HD), HD)], kbuf.at[k], k_load.at[k]))
        v_copies.append(pltpu.make_async_copy(
            cache_hbm.at[:, pl.ds(pl.multiple_of((KVH + g) * HD, HD), HD)], vbuf.at[k], v_load.at[k]))
        k_copies[k].start()
        v_copies[k].start()
    w_copy = pltpu.make_async_copy(w_hbm, wbuf, w_load)
    w_copy.start()

    q_copy.wait()
    row = qrow[...].astype(f32)
    for h in range(H):
        qf[h:h + 1, :] = row[:, h * HD:(h + 1) * HD]
    for slab in range(qdup.shape[0]):
        g = slab % KVH
        qdup[slab] = qf[g * GROUP:(g + 1) * GROUP, :].astype(bf16)
    first_q[ctx] = qdup[pl.ds(z + FIRST_AT, FIRST_N)]
    rest_q[ctx] = qdup[pl.ds(z + REST_AT, REST_N)]

    off_copy.wait()
    start_copy.wait()
    offset = off_smem[0]
    start = start_smem[0]
    first = ctx * span
    eighth = span // 8
    lanes = lax.broadcasted_iota(jnp.int32, (eighth, HD), 1)
    for part in range(8):
        position = first + part * eighth + lax.broadcasted_iota(jnp.int32, (eighth, HD), 0)
        late = jnp.clip(position - offset, 0, QS)
        late = jnp.where(position < start, QS, late)
        fbuf[part * eighth:(part + 1) * eighth, :] = jnp.where(late == lanes, 1.0, 0.0).astype(bf16)
    g_lane = lax.broadcasted_iota(jnp.int32, (ROWS, HD), 1)
    g_row = lax.broadcasted_iota(jnp.int32, (ROWS, HD), 0) % QS
    hide[...] = jnp.where((g_lane > g_row) & (g_lane <= QS), HIDDEN, 0.0).astype(bf16)

    pl.semaphore_wait(barrier, NZ - 1 + NX - 1 + 1)

    def source(i):
        return at_z(-FAR_FIRST[i])

    def two_stage(buf, z_source, z_send, z_recv, x_send, x_recv):
        def along_z(i):
            to = at_z(FAR_FIRST[i])
            return pltpu.make_async_remote_copy(
                z_source(to), buf.at[ctx], z_send.at[i], z_recv.at[i],
                device_id=peer(to, x), device_id_type=MESH)

        def along_x(i, dx):
            own = source(i) * NX + x
            return pltpu.make_async_remote_copy(
                buf.at[own], buf.at[own], x_send.at[i, dx - 1], x_recv.at[i, dx - 1],
                device_id=peer(z, at_x(dx)), device_id_type=MESH)

        def send_own():
            for i in range(NZ - 1):
                along_z(i).start()
            for dx in (2, 1, 3):
                along_x(NZ - 1, dx).start()

        def relay(i):
            along_z(i).wait_recv()
            for dx in (2, 1, 3):
                along_x(i, dx).start()

        def finish():
            for i in range(NZ - 1):
                along_z(i).wait_send()
            for i in range(NZ):
                for dx in range(1, NX):
                    along_x(i, dx).wait_send()

        return send_own, relay, lambda i, dx: along_x(i, dx).wait_recv(), finish

    send_first, relay_first, arrived_first, finish_first = two_stage(
        first_q, lambda to: qdup.at[pl.ds(to + FIRST_AT, FIRST_N)], fz_s, fz_r, fx_s, fx_r)
    send_rest, relay_rest, arrived_rest, finish_rest = two_stage(
        rest_q, lambda to: qdup.at[pl.ds(to + REST_AT, REST_N)], rz_s, rz_r, rx_s, rx_r)

    def unpack(buf, c, heads):
        for j, k in enumerate(heads):
            qg[k, pl.ds(c, GROUP, stride=QS), :] = buf[c, j].astype(f32)

    def take_first(c):
        unpack(first_q, c, FIRST_HEADS)

    def take_rest(c):
        unpack(rest_q, c, REST_HEADS)

    send_first()
    send_rest()
    take_first(ctx)
    take_rest(ctx)
    near_first = list(reversed(range(NZ - 1)))
    lag = 2
    for n in range(NZ - 1 + lag):
        if n < NZ - 1:
            relay_first(near_first[n])
            take_first(source(near_first[n]) * NX + x)
        if n >= lag:
            relay_rest(near_first[n - lag])
            take_rest(source(near_first[n - lag]) * NX + x)
    for i in reversed(range(NZ)):
        for dx in range(1, NX):
            arrived_first(i, dx)
            take_first(source(i) * NX + at_x(-dx))
    for k in FIRST_HEADS:
        qb[k] = qg[k].astype(bf16)

    def wait_rest():
        for i in reversed(range(NZ)):
            for dx in range(1, NX):
                arrived_rest(i, dx)
                take_rest(source(i) * NX + at_x(-dx))
        for k in REST_HEADS:
            qb[k] = qg[k].astype(bf16)

    lane = lax.broadcasted_iota(jnp.int32, (CHUNK, HD), 1)
    line = lax.broadcasted_iota(jnp.int32, (CHUNK, HD), 0)
    diagonal = lane == line
    diagonal_high = lane == line + CHUNK
    low = lax.broadcasted_iota(jnp.int32, (1, HD), 1) < CHUNK

    def x_copies(k, dx):
        to = at_x(dx)
        where = peer(z, to)
        return (
            pltpu.make_async_remote_copy(
                osend.at[k, pl.ds(pl.multiple_of(to * CHUNK, CHUNK), CHUNK), :],
                xbuf.at[k, dx - 1], xs_s.at[k, dx - 1, 0], xs_r.at[k, dx - 1, 0],
                device_id=where, device_id_type=MESH),
            pltpu.make_async_remote_copy(
                ostat.at[k, to, pl.ds(0, 1), :], xstat.at[k, dx - 1, pl.ds(0, 1), :],
                xs_s.at[k, dx - 1, 1], xs_r.at[k, dx - 1, 1],
                device_id=where, device_id_type=MESH),
        )

    def z_copies(k, dz):
        where = peer(at_z(dz), x)
        return (
            pltpu.make_async_remote_copy(
                zsend.at[k], zbuf.at[k], zs_s.at[k, 0], zs_r.at[k, 0],
                device_id=where, device_id_type=MESH),
            pltpu.make_async_remote_copy(
                zsstat.at[k, pl.ds(0, 1), :], zstat.at[k, pl.ds(0, 1), :],
                zs_s.at[k, 1], zs_r.at[k, 1], device_id=where, device_id_type=MESH),
        )

    def join(parts):
        top = functools.reduce(jnp.maximum, [stat for stat, _ in parts])
        total = jnp.zeros_like(top)
        mixed = jnp.zeros((CHUNK, HD), f32)
        for stat, numerator in parts:
            factor = jnp.exp2(stat - top)
            total = total + pltpu.roll(factor, CHUNK, 1) * stat
            column = jnp.sum(
                jnp.where(diagonal, jnp.broadcast_to(factor, (CHUNK, HD)), 0.0),
                axis=1, keepdims=True)
            mixed = mixed + column * numerator.astype(f32)
        return jnp.where(low, top, total), mixed

    own_rows = pl.ds(pl.multiple_of(x * CHUNK, CHUNK), CHUNK)

    def join_x(k):
        parts = [(ostat[k, x, 0:1, :], osend[k, own_rows, :])]
        for dx in range(1, NX):
            for copy in x_copies(k, dx):
                copy.wait_recv()
            parts.append((xstat[k, dx - 1, 0:1, :], xbuf[k, dx - 1]))
        stat, mixed = join(parts)
        zsend[k] = mixed.astype(bf16)
        zsstat[k, 0:1, :] = stat
        if FAR_FIRST[k] != 0:
            for copy in z_copies(k, FAR_FIRST[k]):
                copy.start()

    scores = (s_even, s_odd)
    rounded = (p_even, p_odd)
    tile, block = 256, 16
    per = CHUNK // block
    b_lane = lax.broadcasted_iota(jnp.int32, (block, HD), 1)
    b_line = lax.broadcasted_iota(jnp.int32, (block, HD), 0)

    def score_tile(k, c):
        rows = slice(c * tile, (c + 1) * tile)
        query = jnp.concatenate([qb[k], hide[...]], axis=1)
        keys = jnp.concatenate([kbuf[k, rows, :], fbuf[rows, :]], axis=1)
        scores[k % 2][:, rows] = lax.dot_general(
            query, keys, (((1,), (1,)), ((), ())), preferred_element_type=f32)

    def soften(k, r, stat):
        rows = slice(r * block, (r + 1) * block)
        score = scores[k % 2][rows, :]
        top = jnp.max(score, axis=1, keepdims=True)
        weight = jnp.exp2((score - top) * SCALE2)
        total = jnp.sum(weight, axis=1, keepdims=True)
        rounded[k % 2][rows, :] = weight.astype(bf16)
        at = b_lane - b_line - (r % per) * block
        part = jnp.where(at == 0, top * SCALE2, 0.0) + jnp.where(at == CHUNK, total, 0.0)
        part = part[:8] + part[8:]
        stat = part if r % per == 0 else stat + part
        if r % per == per - 1:
            ostat[k, r // per, 0:1, :] = jnp.sum(stat, axis=0, keepdims=True)
        return stat

    def value_tile(k, c):
        rows = slice(c * tile, (c + 1) * tile)
        term = jnp.dot(rounded[k % 2][:, rows], vbuf[k, rows, :], preferred_element_type=f32)
        if c == 0:
            partial[k % 2] = term
        elif c < tiles - 1:
            partial[k % 2] = partial[k % 2] + term
        else:
            osend[k] = (partial[k % 2] + term).astype(bf16)

    tiles = span // tile
    for k in range(KVH):
        k_copies[k].wait()
        v_copies[k].wait()
    for i in range(KVH + 2):
        if i == FIRST_N:
            wait_rest()
        stat = None
        for r in range(ROWS // block):
            if 1 <= i <= KVH:
                stat = soften(i - 1, r, stat)
            if r % 2 == 0 and i < KVH:
                score_tile(i, r // 2)
            if r % 2 == 1 and i >= 2:
                value_tile(i - 2, r // 2)
        for k in SEND_AFTER.get(i, ()):
            for dx in (2, 1, 3):
                for copy in x_copies(k, dx):
                    copy.start()
        for k in JOIN_AFTER.get(i, ()):
            join_x(k)

    own = NZ - 1
    parts = [(zsstat[own, 0:1, :], zsend[own])]
    for k in range(NZ - 1):
        for copy in z_copies(k, FAR_FIRST[k]):
            copy.wait_recv()
        parts.append((zstat[k, 0:1, :], zbuf[k]))
    stat, mixed = join(parts)
    divisor = jnp.sum(
        jnp.where(diagonal_high, jnp.broadcast_to(stat, (CHUNK, HD)), 0.0), axis=1, keepdims=True)
    mixed = mixed / divisor
    abuf[ctx] = jnp.concatenate([mixed[:QS], mixed[QS:]], axis=1).astype(bf16)

    def chunk_copy(c, send, recv, where):
        return pltpu.make_async_remote_copy(
            abuf.at[c], abuf.at[c], send, recv, device_id=where, device_id_type=MESH)

    def a_z(i):
        return chunk_copy(ctx, az_s.at[i], az_r.at[i], peer(at_z(FAR_FIRST[i]), x))

    def a_x(i, dx):
        return chunk_copy(
            source(i) * NX + x, ax_s.at[i, dx - 1], ax_r.at[i, dx - 1], peer(z, at_x(dx)))

    def a_near(i, dx):
        return chunk_copy(
            z * NX + at_x(-dx), ax_s.at[i, dx - 1], ax_r.at[i, dx - 1],
            peer(at_z(FAR_FIRST[i]), x))

    def term(c):
        return jnp.dot(
            abuf[c], wbuf[pl.ds(pl.multiple_of(c * 2 * HD, 2 * HD), 2 * HD), :],
            preferred_element_type=f32)

    mine = NZ - 1
    for i in range(mine):
        a_z(i).start()
    for dx in (2, 1, 3):
        a_x(mine, dx).start()
    w_copy.wait()
    projected = term(ctx)
    for dx in (1, 3, 2):
        a_x(mine, dx).wait_recv()
        for i in Z_NEAR:
            a_near(i, dx).start()
        projected = projected + term(z * NX + at_x(-dx))
    for i in Z_FAR:
        a_z(i).wait_recv()
        for dx in (2, 1, 3):
            a_x(i, dx).start()
        projected = projected + term(source(i) * NX + x)
    for i in Z_NEAR:
        a_z(i).wait_recv()
        projected = projected + term(source(i) * NX + x)
        for dx in (1, 3, 2):
            a_near(i, dx).wait_recv()
            projected = projected + term(source(i) * NX + at_x(-dx))
    for i in Z_FAR:
        for dx in (1, 3, 2):
            a_x(i, dx).wait_recv()
            projected = projected + term(source(i) * NX + at_x(-dx))

    def finish_a():
        for i in range(mine):
            a_z(i).wait_send()
            for dx in range(1, NX):
                (a_near if i in Z_NEAR else a_x)(i, dx).wait_send()
        for dx in range(1, NX):
            a_x(mine, dx).wait_send()

    ysend[...] = projected.astype(bf16)
    y_copy = pltpu.make_async_remote_copy(
        ysend, out_ref, y_s.at[0], y_r.at[0],
        device_id={"segment": after, "ctx": ctx}, device_id_type=MESH)
    y_copy.start()
    finish_first()
    finish_rest()
    finish_a()
    for k, dz in enumerate(FAR_FIRST):
        for dx in range(1, NX):
            for copy in x_copies(k, dx):
                copy.wait_send()
        if dz != 0:
            for copy in z_copies(k, dz):
                copy.wait_send()
    y_copy.wait()


def per_device(queries, cache, out_weight, offsets, starts):
    span = cache.shape[0]
    columns = out_weight.shape[1]
    bf16, f32 = jnp.bfloat16, jnp.float32
    dma = pltpu.SemaphoreType.DMA
    hop = [dma((NZ - 1,)), dma((NZ - 1,)), dma((NZ, NX - 1)), dma((NZ, NX - 1))]
    return pl.pallas_call(
        kernel,
        out_shape=jax.ShapeDtypeStruct((QS, columns), bf16),
        in_specs=[pl.BlockSpec(memory_space=pltpu.HBM)] * 5,
        out_specs=pl.BlockSpec(memory_space=pltpu.VMEM),
        scratch_shapes=[
            pltpu.SMEM((1,), jnp.int32),
            pltpu.SMEM((1,), jnp.int32),
            pltpu.VMEM((1, H * HD), bf16),
            pltpu.VMEM((H, HD), f32),
            pltpu.VMEM((REST_AT + REST_N + NZ - 1, GROUP, HD), bf16),
            pltpu.VMEM((QS, FIRST_N, GROUP, HD), bf16),
            pltpu.VMEM((QS, REST_N, GROUP, HD), bf16),
            pltpu.VMEM((KVH, ROWS, HD), f32),
            pltpu.VMEM((KVH, ROWS, HD), bf16),
            pltpu.VMEM((ROWS, HD), bf16),
            pltpu.VMEM((span, HD), bf16),
            pltpu.VMEM((KVH, span, HD), bf16),
            pltpu.VMEM((KVH, span, HD), bf16),
            pltpu.VMEM((H * HD, columns), bf16),
            pltpu.VMEM((ROWS, span), f32),
            pltpu.VMEM((ROWS, span), f32),
            pltpu.VMEM((ROWS, span), bf16),
            pltpu.VMEM((ROWS, span), bf16),
            pltpu.VMEM((2, ROWS, HD), f32),
            pltpu.VMEM((KVH, ROWS, HD), bf16),
            pltpu.VMEM((KVH, NX, 8, HD), f32),
            pltpu.VMEM((KVH, NX - 1, CHUNK, HD), bf16),
            pltpu.VMEM((KVH, NX - 1, 8, HD), f32),
            pltpu.VMEM((NZ, CHUNK, HD), bf16),
            pltpu.VMEM((NZ, 8, HD), f32),
            pltpu.VMEM((NZ, CHUNK, HD), bf16),
            pltpu.VMEM((NZ, 8, HD), f32),
            pltpu.VMEM((QS, QS, 2 * HD), bf16),
            pltpu.VMEM((QS, columns), bf16),
            dma((2,)), dma, dma((KVH,)), dma((KVH,)), dma,
            *hop, *hop,
            dma((KVH, NX - 1, 2)), dma((KVH, NX - 1, 2)),
            dma((NZ - 1, 2)), dma((NZ - 1, 2)),
            *hop,
            dma((1,)), dma((1,)),
        ],
        compiler_params=pltpu.CompilerParams(collective_id=0, has_side_effects=True, vmem_limit_bytes=VMEM_LIMIT),
        name="section_attention",
    )(offsets, starts, *[
        pltpu.with_memory_space_constraint(a, pltpu.HBM) for a in (queries, cache, out_weight)])


def solution(mesh):
    in_specs = (
        P(("segment", "ctx"), None),
        P(("segment", "ctx"), None),
        P("segment", "ctx"),
        P("segment"),
        P("segment"),
    )
    out_specs = P("segment", "ctx")
    return jax.shard_map(
        per_device, mesh=mesh, in_specs=in_specs, out_specs=out_specs, check_vma=False
    )
```

```python
import functools

import jax
import jax.numpy as jnp
from jax import lax
from jax.experimental import pallas as pl
from jax.experimental.pallas import tpu as pltpu
from jax.sharding import PartitionSpec as P

VMEM_LIMIT = 40 * 1024 * 1024
H = 64
KVH = 8
HD = 128
GROUP = H // KVH
NX = 4
NZ = 8
QS = NX * NZ
ROWS = QS * GROUP
CHUNK = ROWS // NX
SCALE2 = HD ** (-0.5) * 1.4426950408889634
HIDDEN = -1e30
MESH = pl.DeviceIdType.MESH
FAR_FIRST = (4, 3, -3, 2, -2, 1, -1, 0)
Z_NEAR = (6, 5)
Z_FAR = (4, 3, 2, 1, 0)
FIRST_AT, FIRST_N, FIRST_HEADS = 3, 2, (1, 0)
REST_AT, REST_N, REST_HEADS = 5, 6, (2, 4, 6, 7, 5, 3)
SEND_AFTER = {3: (0, 1), 5: (2, 3), 7: (4, 5), 9: (6, 7)}
JOIN_AFTER = {9: (0, 1, 2, 3, 4, 5, 6, 7)}


def kernel(off_hbm, start_hbm, q_hbm, cache_hbm, w_hbm, out_ref, off_smem, start_smem, qrow, qf,
           qdup, first_q, rest_q, qg, qb, hide, fbuf, kbuf, vbuf, wbuf, s_even, s_odd, p_even,
           p_odd, partial, osend, ostat, xbuf, xstat, zsend, zsstat, zbuf, zstat, abuf, ysend, small_load,
           q_load, k_load, v_load, w_load, fz_s, fz_r, fx_s, fx_r, rz_s, rz_r, rx_s, rx_r, xs_s,
           xs_r, zs_s, zs_r, az_s, az_r, ax_s, ax_r, y_s, y_r):
    segment = lax.axis_index("segment")
    ctx = lax.axis_index("ctx")
    z = ctx // NX
    x = ctx % NX
    n_seg = lax.axis_size("segment")
    span = cache_hbm.shape[0]
    bf16, f32 = jnp.bfloat16, jnp.float32

    def at_z(step):
        return (z + step + NZ) % NZ

    def at_x(step):
        return (x + step + NX) % NX

    def peer(zz, xx):
        return {"segment": segment, "ctx": zz * NX + xx}

    barrier = pltpu.get_barrier_semaphore()
    for step in range(1, NZ):
        pl.semaphore_signal(barrier, inc=1, device_id=peer(at_z(step), x), device_id_type=MESH)
    for step in range(1, NX):
        pl.semaphore_signal(barrier, inc=1, device_id=peer(z, at_x(step)), device_id_type=MESH)
    before = (segment + n_seg - 1) % n_seg
    after = (segment + 1) % n_seg
    pl.semaphore_signal(
        barrier, inc=1, device_id={"segment": before, "ctx": ctx}, device_id_type=MESH
    )

    q_copy = pltpu.make_async_copy(q_hbm, qrow, q_load)
    q_copy.start()
    off_copy = pltpu.make_async_copy(off_hbm, off_smem, small_load.at[0])
    start_copy = pltpu.make_async_copy(start_hbm, start_smem, small_load.at[1])
    off_copy.start()
    start_copy.start()
    k_copies, v_copies = [], []
    for k, dz in enumerate(FAR_FIRST):
        g = at_z(dz)
        k_copies.append(pltpu.make_async_copy(
            cache_hbm.at[:, pl.ds(pl.multiple_of(g * HD, HD), HD)], kbuf.at[k], k_load.at[k]))
        v_copies.append(pltpu.make_async_copy(
            cache_hbm.at[:, pl.ds(pl.multiple_of((KVH + g) * HD, HD), HD)], vbuf.at[k], v_load.at[k]))
        k_copies[k].start()
        v_copies[k].start()
    w_copy = pltpu.make_async_copy(w_hbm, wbuf, w_load)
    w_copy.start()

    q_copy.wait()
    row = qrow[...].astype(f32)
    for h in range(H):
        qf[h:h + 1, :] = row[:, h * HD:(h + 1) * HD]
    for slab in range(qdup.shape[0]):
        g = slab % KVH
        qdup[slab] = qf[g * GROUP:(g + 1) * GROUP, :].astype(bf16)
    first_q[ctx] = qdup[pl.ds(z + FIRST_AT, FIRST_N)]
    rest_q[ctx] = qdup[pl.ds(z + REST_AT, REST_N)]

    off_copy.wait()
    start_copy.wait()
    offset = off_smem[0]
    start = start_smem[0]
    first = ctx * span
    eighth = span // 8
    lanes = lax.broadcasted_iota(jnp.int32, (eighth, HD), 1)
    for part in range(8):
        position = first + part * eighth + lax.broadcasted_iota(jnp.int32, (eighth, HD), 0)
        late = jnp.clip(position - offset, 0, QS)
        late = jnp.where(position < start, QS, late)
        fbuf[part * eighth:(part + 1) * eighth, :] = jnp.where(late == lanes, 1.0, 0.0).astype(bf16)
    g_lane = lax.broadcasted_iota(jnp.int32, (ROWS, HD), 1)
    g_row = lax.broadcasted_iota(jnp.int32, (ROWS, HD), 0) % QS
    hide[...] = jnp.where((g_lane > g_row) & (g_lane <= QS), HIDDEN, 0.0).astype(bf16)

    pl.semaphore_wait(barrier, NZ - 1 + NX - 1 + 1)

    def source(i):
        return at_z(-FAR_FIRST[i])

    def two_stage(buf, z_source, z_send, z_recv, x_send, x_recv):
        def along_z(i):
            to = at_z(FAR_FIRST[i])
            return pltpu.make_async_remote_copy(
                z_source(to), buf.at[ctx], z_send.at[i], z_recv.at[i],
                device_id=peer(to, x), device_id_type=MESH)

        def along_x(i, dx):
            own = source(i) * NX + x
            return pltpu.make_async_remote_copy(
                buf.at[own], buf.at[own], x_send.at[i, dx - 1], x_recv.at[i, dx - 1],
                device_id=peer(z, at_x(dx)), device_id_type=MESH)

        def send_own():
            for i in range(NZ - 1):
                along_z(i).start()
            for dx in (2, 1, 3):
                along_x(NZ - 1, dx).start()

        def relay(i):
            along_z(i).wait_recv()
            for dx in (2, 1, 3):
                along_x(i, dx).start()

        def finish():
            for i in range(NZ - 1):
                along_z(i).wait_send()
            for i in range(NZ):
                for dx in range(1, NX):
                    along_x(i, dx).wait_send()

        return send_own, relay, lambda i, dx: along_x(i, dx).wait_recv(), finish

    send_first, relay_first, arrived_first, finish_first = two_stage(
        first_q, lambda to: qdup.at[pl.ds(to + FIRST_AT, FIRST_N)], fz_s, fz_r, fx_s, fx_r)
    send_rest, relay_rest, arrived_rest, finish_rest = two_stage(
        rest_q, lambda to: qdup.at[pl.ds(to + REST_AT, REST_N)], rz_s, rz_r, rx_s, rx_r)

    def unpack(buf, c, heads):
        for j, k in enumerate(heads):
            qg[k, pl.ds(c, GROUP, stride=QS), :] = buf[c, j].astype(f32)

    def take_first(c):
        unpack(first_q, c, FIRST_HEADS)

    def take_rest(c):
        unpack(rest_q, c, REST_HEADS)

    send_first()
    send_rest()
    take_first(ctx)
    take_rest(ctx)
    near_first = list(reversed(range(NZ - 1)))
    lag = 7
    for n in range(NZ - 1 + lag):
        if n < NZ - 1:
            relay_first(near_first[n])
            take_first(source(near_first[n]) * NX + x)
        if n >= lag:
            relay_rest(near_first[n - lag])
            take_rest(source(near_first[n - lag]) * NX + x)
    for i in reversed(range(NZ)):
        for dx in range(1, NX):
            arrived_first(i, dx)
            take_first(source(i) * NX + at_x(-dx))
    for k in FIRST_HEADS:
        qb[k] = qg[k].astype(bf16)

    def wait_rest():
        for i in reversed(range(NZ)):
            for dx in range(1, NX):
                arrived_rest(i, dx)
                take_rest(source(i) * NX + at_x(-dx))
        for k in REST_HEADS:
            qb[k] = qg[k].astype(bf16)

    lane = lax.broadcasted_iota(jnp.int32, (CHUNK, HD), 1)
    line = lax.broadcasted_iota(jnp.int32, (CHUNK, HD), 0)
    diagonal = lane == line
    diagonal_high = lane == line + CHUNK
    low = lax.broadcasted_iota(jnp.int32, (1, HD), 1) < CHUNK

    def x_copies(k, dx):
        to = at_x(dx)
        where = peer(z, to)
        return (
            pltpu.make_async_remote_copy(
                osend.at[k, pl.ds(pl.multiple_of(to * CHUNK, CHUNK), CHUNK), :],
                xbuf.at[k, dx - 1], xs_s.at[k, dx - 1, 0], xs_r.at[k, dx - 1, 0],
                device_id=where, device_id_type=MESH),
            pltpu.make_async_remote_copy(
                ostat.at[k, to, pl.ds(0, 1), :], xstat.at[k, dx - 1, pl.ds(0, 1), :],
                xs_s.at[k, dx - 1, 1], xs_r.at[k, dx - 1, 1],
                device_id=where, device_id_type=MESH),
        )

    def z_copies(k, dz):
        where = peer(at_z(dz), x)
        return (
            pltpu.make_async_remote_copy(
                zsend.at[k], zbuf.at[k], zs_s.at[k, 0], zs_r.at[k, 0],
                device_id=where, device_id_type=MESH),
            pltpu.make_async_remote_copy(
                zsstat.at[k, pl.ds(0, 1), :], zstat.at[k, pl.ds(0, 1), :],
                zs_s.at[k, 1], zs_r.at[k, 1], device_id=where, device_id_type=MESH),
        )

    def join(parts):
        top = functools.reduce(jnp.maximum, [stat for stat, _ in parts])
        total = jnp.zeros_like(top)
        mixed = jnp.zeros((CHUNK, HD), f32)
        for stat, numerator in parts:
            factor = jnp.exp2(stat - top)
            total = total + pltpu.roll(factor, CHUNK, 1) * stat
            column = jnp.sum(
                jnp.where(diagonal, jnp.broadcast_to(factor, (CHUNK, HD)), 0.0),
                axis=1, keepdims=True)
            mixed = mixed + column * numerator.astype(f32)
        return jnp.where(low, top, total), mixed

    own_rows = pl.ds(pl.multiple_of(x * CHUNK, CHUNK), CHUNK)

    def join_x(k):
        parts = [(ostat[k, x, 0:1, :], osend[k, own_rows, :])]
        for dx in range(1, NX):
            for copy in x_copies(k, dx):
                copy.wait_recv()
            parts.append((xstat[k, dx - 1, 0:1, :], xbuf[k, dx - 1]))
        stat, mixed = join(parts)
        zsend[k] = mixed.astype(bf16)
        zsstat[k, 0:1, :] = stat
        if FAR_FIRST[k] != 0:
            for copy in z_copies(k, FAR_FIRST[k]):
                copy.start()

    scores = (s_even, s_odd)
    rounded = (p_even, p_odd)
    tile, block = 256, 16
    per = CHUNK // block
    b_lane = lax.broadcasted_iota(jnp.int32, (block, HD), 1)
    b_line = lax.broadcasted_iota(jnp.int32, (block, HD), 0)

    def score_tile(k, c):
        rows = slice(c * tile, (c + 1) * tile)
        query = jnp.concatenate([qb[k], hide[...]], axis=1)
        keys = jnp.concatenate([kbuf[k, rows, :], fbuf[rows, :]], axis=1)
        scores[k % 2][:, rows] = lax.dot_general(
            query, keys, (((1,), (1,)), ((), ())), preferred_element_type=f32)

    def soften(k, r, stat):
        rows = slice(r * block, (r + 1) * block)
        score = scores[k % 2][rows, :]
        top = jnp.max(score, axis=1, keepdims=True)
        weight = jnp.exp2((score - top) * SCALE2)
        total = jnp.sum(weight, axis=1, keepdims=True)
        rounded[k % 2][rows, :] = weight.astype(bf16)
        at = b_lane - b_line - (r % per) * block
        part = jnp.where(at == 0, top * SCALE2, 0.0) + jnp.where(at == CHUNK, total, 0.0)
        part = part[:8] + part[8:]
        stat = part if r % per == 0 else stat + part
        if r % per == per - 1:
            ostat[k, r // per, 0:1, :] = jnp.sum(stat, axis=0, keepdims=True)
        return stat

    def value_tile(k, c):
        rows = slice(c * tile, (c + 1) * tile)
        term = jnp.dot(rounded[k % 2][:, rows], vbuf[k, rows, :], preferred_element_type=f32)
        if c == 0:
            partial[k % 2] = term
        elif c < tiles - 1:
            partial[k % 2] = partial[k % 2] + term
        else:
            osend[k] = (partial[k % 2] + term).astype(bf16)

    tiles = span // tile
    for k in range(KVH):
        k_copies[k].wait()
        v_copies[k].wait()
    for i in range(KVH + 2):
        if i == FIRST_N:
            wait_rest()
        stat = None
        for r in range(ROWS // block):
            if 1 <= i <= KVH:
                stat = soften(i - 1, r, stat)
            if r % 2 == 0 and i < KVH:
                score_tile(i, r // 2)
            if r % 2 == 1 and i >= 2:
                value_tile(i - 2, r // 2)
        for k in SEND_AFTER.get(i, ()):
            for dx in (2, 1, 3):
                for copy in x_copies(k, dx):
                    copy.start()
        for k in JOIN_AFTER.get(i, ()):
            join_x(k)

    own = NZ - 1
    parts = [(zsstat[own, 0:1, :], zsend[own])]
    for k in range(NZ - 1):
        for copy in z_copies(k, FAR_FIRST[k]):
            copy.wait_recv()
        parts.append((zstat[k, 0:1, :], zbuf[k]))
    stat, mixed = join(parts)
    divisor = jnp.sum(
        jnp.where(diagonal_high, jnp.broadcast_to(stat, (CHUNK, HD)), 0.0), axis=1, keepdims=True)
    mixed = mixed / divisor
    abuf[ctx] = jnp.concatenate([mixed[:QS], mixed[QS:]], axis=1).astype(bf16)

    def chunk_copy(c, send, recv, where):
        return pltpu.make_async_remote_copy(
            abuf.at[c], abuf.at[c], send, recv, device_id=where, device_id_type=MESH)

    def a_z(i):
        return chunk_copy(ctx, az_s.at[i], az_r.at[i], peer(at_z(FAR_FIRST[i]), x))

    def a_x(i, dx):
        return chunk_copy(
            source(i) * NX + x, ax_s.at[i, dx - 1], ax_r.at[i, dx - 1], peer(z, at_x(dx)))

    def a_near(i, dx):
        return chunk_copy(
            z * NX + at_x(-dx), ax_s.at[i, dx - 1], ax_r.at[i, dx - 1],
            peer(at_z(FAR_FIRST[i]), x))

    def term(c):
        return jnp.dot(
            abuf[c], wbuf[pl.ds(pl.multiple_of(c * 2 * HD, 2 * HD), 2 * HD), :],
            preferred_element_type=f32)

    mine = NZ - 1
    for i in range(mine):
        a_z(i).start()
    for dx in (2, 1, 3):
        a_x(mine, dx).start()
    w_copy.wait()
    projected = term(ctx)
    for dx in (1, 3, 2):
        a_x(mine, dx).wait_recv()
        for i in Z_NEAR:
            a_near(i, dx).start()
        projected = projected + term(z * NX + at_x(-dx))
    for i in Z_FAR:
        a_z(i).wait_recv()
        for dx in (2, 1, 3):
            a_x(i, dx).start()
        projected = projected + term(source(i) * NX + x)
    for i in Z_NEAR:
        a_z(i).wait_recv()
        projected = projected + term(source(i) * NX + x)
        for dx in (1, 3, 2):
            a_near(i, dx).wait_recv()
            projected = projected + term(source(i) * NX + at_x(-dx))
    for i in Z_FAR:
        for dx in (1, 3, 2):
            a_x(i, dx).wait_recv()
            projected = projected + term(source(i) * NX + at_x(-dx))

    def finish_a():
        for i in range(mine):
            a_z(i).wait_send()
            for dx in range(1, NX):
                (a_near if i in Z_NEAR else a_x)(i, dx).wait_send()
        for dx in range(1, NX):
            a_x(mine, dx).wait_send()

    ysend[...] = projected.astype(bf16)
    y_copy = pltpu.make_async_remote_copy(
        ysend, out_ref, y_s.at[0], y_r.at[0],
        device_id={"segment": after, "ctx": ctx}, device_id_type=MESH)
    y_copy.start()
    finish_first()
    finish_rest()
    finish_a()
    for k, dz in enumerate(FAR_FIRST):
        for dx in range(1, NX):
            for copy in x_copies(k, dx):
                copy.wait_send()
        if dz != 0:
            for copy in z_copies(k, dz):
                copy.wait_send()
    y_copy.wait()


def per_device(queries, cache, out_weight, offsets, starts):
    span = cache.shape[0]
    columns = out_weight.shape[1]
    bf16, f32 = jnp.bfloat16, jnp.float32
    dma = pltpu.SemaphoreType.DMA
    hop = [dma((NZ - 1,)), dma((NZ - 1,)), dma((NZ, NX - 1)), dma((NZ, NX - 1))]
    return pl.pallas_call(
        kernel,
        out_shape=jax.ShapeDtypeStruct((QS, columns), bf16),
        in_specs=[pl.BlockSpec(memory_space=pltpu.HBM)] * 5,
        out_specs=pl.BlockSpec(memory_space=pltpu.VMEM),
        scratch_shapes=[
            pltpu.SMEM((1,), jnp.int32),
            pltpu.SMEM((1,), jnp.int32),
            pltpu.VMEM((1, H * HD), bf16),
            pltpu.VMEM((H, HD), f32),
            pltpu.VMEM((REST_AT + REST_N + NZ - 1, GROUP, HD), bf16),
            pltpu.VMEM((QS, FIRST_N, GROUP, HD), bf16),
            pltpu.VMEM((QS, REST_N, GROUP, HD), bf16),
            pltpu.VMEM((KVH, ROWS, HD), f32),
            pltpu.VMEM((KVH, ROWS, HD), bf16),
            pltpu.VMEM((ROWS, HD), bf16),
            pltpu.VMEM((span, HD), bf16),
            pltpu.VMEM((KVH, span, HD), bf16),
            pltpu.VMEM((KVH, span, HD), bf16),
            pltpu.VMEM((H * HD, columns), bf16),
            pltpu.VMEM((ROWS, span), f32),
            pltpu.VMEM((ROWS, span), f32),
            pltpu.VMEM((ROWS, span), bf16),
            pltpu.VMEM((ROWS, span), bf16),
            pltpu.VMEM((2, ROWS, HD), f32),
            pltpu.VMEM((KVH, ROWS, HD), bf16),
            pltpu.VMEM((KVH, NX, 8, HD), f32),
            pltpu.VMEM((KVH, NX - 1, CHUNK, HD), bf16),
            pltpu.VMEM((KVH, NX - 1, 8, HD), f32),
            pltpu.VMEM((NZ, CHUNK, HD), bf16),
            pltpu.VMEM((NZ, 8, HD), f32),
            pltpu.VMEM((NZ, CHUNK, HD), bf16),
            pltpu.VMEM((NZ, 8, HD), f32),
            pltpu.VMEM((QS, QS, 2 * HD), bf16),
            pltpu.VMEM((QS, columns), bf16),
            dma((2,)), dma, dma((KVH,)), dma((KVH,)), dma,
            *hop, *hop,
            dma((KVH, NX - 1, 2)), dma((KVH, NX - 1, 2)),
            dma((NZ - 1, 2)), dma((NZ - 1, 2)),
            *hop,
            dma((1,)), dma((1,)),
        ],
        compiler_params=pltpu.CompilerParams(collective_id=0, has_side_effects=True, vmem_limit_bytes=VMEM_LIMIT),
        name="section_attention",
    )(offsets, starts, *[
        pltpu.with_memory_space_constraint(a, pltpu.HBM) for a in (queries, cache, out_weight)])


def solution(mesh):
    in_specs = (
        P(("segment", "ctx"), None),
        P(("segment", "ctx"), None),
        P("segment", "ctx"),
        P("segment"),
        P("segment"),
    )
    out_specs = P("segment", "ctx")
    return jax.shard_map(
        per_device, mesh=mesh, in_specs=in_specs, out_specs=out_specs, check_vma=False
    )
```

```python
import functools

import jax
import jax.numpy as jnp
from jax import lax
from jax.experimental import pallas as pl
from jax.experimental.pallas import tpu as pltpu
from jax.sharding import PartitionSpec as P

VMEM_LIMIT = 40 * 1024 * 1024
H = 64
KVH = 8
HD = 128
GROUP = H // KVH
NX = 4
NZ = 8
QS = NX * NZ
ROWS = QS * GROUP
CHUNK = ROWS // NX
SCALE2 = HD ** (-0.5) * 1.4426950408889634
HIDDEN = -1e30
MESH = pl.DeviceIdType.MESH
FAR_FIRST = (4, 3, -3, 2, -2, 1, -1, 0)
Z_NEAR = (6, 5)
Z_FAR = (4, 3, 2, 1, 0)
FIRST_AT, FIRST_N, FIRST_HEADS = 3, 2, (1, 0)
REST_AT, REST_N, REST_HEADS = 5, 6, (2, 4, 6, 7, 5, 3)
SEND_AFTER = {3: (0, 1), 5: (2, 3), 7: (4, 5), 9: (6, 7)}
JOIN_AFTER = {9: (0, 1, 2, 3, 4, 5, 6, 7)}


def kernel(off_hbm, start_hbm, q_hbm, cache_hbm, w_hbm, out_ref, off_smem, start_smem, qrow, qf,
           qdup, first_q, rest_q, qg, qb, hide, fbuf, kbuf, vbuf, wbuf, s_even, s_odd, p_even,
           p_odd, partial, osend, ostat, xbuf, xstat, zsend, zsstat, zbuf, zstat, abuf, ysend, small_load,
           q_load, k_load, v_load, w_load, fz_s, fz_r, fx_s, fx_r, rz_s, rz_r, rx_s, rx_r, xs_s,
           xs_r, zs_s, zs_r, az_s, az_r, ax_s, ax_r, y_s, y_r):
    segment = lax.axis_index("segment")
    ctx = lax.axis_index("ctx")
    z = ctx // NX
    x = ctx % NX
    n_seg = lax.axis_size("segment")
    span = cache_hbm.shape[0]
    bf16, f32 = jnp.bfloat16, jnp.float32

    def at_z(step):
        return (z + step + NZ) % NZ

    def at_x(step):
        return (x + step + NX) % NX

    def peer(zz, xx):
        return {"segment": segment, "ctx": zz * NX + xx}

    barrier = pltpu.get_barrier_semaphore()
    for step in range(1, NZ):
        pl.semaphore_signal(barrier, inc=1, device_id=peer(at_z(step), x), device_id_type=MESH)
    for step in range(1, NX):
        pl.semaphore_signal(barrier, inc=1, device_id=peer(z, at_x(step)), device_id_type=MESH)
    before = (segment + n_seg - 1) % n_seg
    after = (segment + 1) % n_seg
    pl.semaphore_signal(
        barrier, inc=1, device_id={"segment": before, "ctx": ctx}, device_id_type=MESH
    )

    q_copy = pltpu.make_async_copy(q_hbm, qrow, q_load)
    q_copy.start()
    off_copy = pltpu.make_async_copy(off_hbm, off_smem, small_load.at[0])
    start_copy = pltpu.make_async_copy(start_hbm, start_smem, small_load.at[1])
    off_copy.start()
    start_copy.start()
    k_copies, v_copies = [], []
    for k, dz in enumerate(FAR_FIRST):
        g = at_z(dz)
        k_copies.append(pltpu.make_async_copy(
            cache_hbm.at[:, pl.ds(pl.multiple_of(g * HD, HD), HD)], kbuf.at[k], k_load.at[k]))
        v_copies.append(pltpu.make_async_copy(
            cache_hbm.at[:, pl.ds(pl.multiple_of((KVH + g) * HD, HD), HD)], vbuf.at[k], v_load.at[k]))
        k_copies[k].start()
        v_copies[k].start()
    w_copy = pltpu.make_async_copy(w_hbm, wbuf, w_load)
    w_copy.start()

    q_copy.wait()
    row = qrow[...].astype(f32)
    for h in range(H):
        qf[h:h + 1, :] = row[:, h * HD:(h + 1) * HD]
    for slab in range(qdup.shape[0]):
        g = slab % KVH
        qdup[slab] = qf[g * GROUP:(g + 1) * GROUP, :].astype(bf16)
    first_q[ctx] = qdup[pl.ds(z + FIRST_AT, FIRST_N)]
    rest_q[ctx] = qdup[pl.ds(z + REST_AT, REST_N)]

    off_copy.wait()
    start_copy.wait()
    offset = off_smem[0]
    start = start_smem[0]
    first = ctx * span
    eighth = span // 8
    lanes = lax.broadcasted_iota(jnp.int32, (eighth, HD), 1)
    for part in range(8):
        position = first + part * eighth + lax.broadcasted_iota(jnp.int32, (eighth, HD), 0)
        late = jnp.clip(position - offset, 0, QS)
        late = jnp.where(position < start, QS, late)
        fbuf[part * eighth:(part + 1) * eighth, :] = jnp.where(late == lanes, 1.0, 0.0).astype(bf16)
    g_lane = lax.broadcasted_iota(jnp.int32, (ROWS, HD), 1)
    g_row = lax.broadcasted_iota(jnp.int32, (ROWS, HD), 0) % QS
    hide[...] = jnp.where((g_lane > g_row) & (g_lane <= QS), HIDDEN, 0.0).astype(bf16)

    pl.semaphore_wait(barrier, NZ - 1 + NX - 1 + 1)

    def source(i):
        return at_z(-FAR_FIRST[i])

    def two_stage(buf, z_source, z_send, z_recv, x_send, x_recv):
        def along_z(i):
            to = at_z(FAR_FIRST[i])
            return pltpu.make_async_remote_copy(
                z_source(to), buf.at[ctx], z_send.at[i], z_recv.at[i],
                device_id=peer(to, x), device_id_type=MESH)

        def along_x(i, dx):
            own = source(i) * NX + x
            return pltpu.make_async_remote_copy(
                buf.at[own], buf.at[own], x_send.at[i, dx - 1], x_recv.at[i, dx - 1],
                device_id=peer(z, at_x(dx)), device_id_type=MESH)

        def send_own():
            for i in range(NZ - 1):
                along_z(i).start()
            for dx in (2, 1, 3):
                along_x(NZ - 1, dx).start()

        def relay(i):
            along_z(i).wait_recv()
            for dx in (2, 1, 3):
                along_x(i, dx).start()

        def finish():
            for i in range(NZ - 1):
                along_z(i).wait_send()
            for i in range(NZ):
                for dx in range(1, NX):
                    along_x(i, dx).wait_send()

        return send_own, relay, lambda i, dx: along_x(i, dx).wait_recv(), finish

    send_first, relay_first, arrived_first, finish_first = two_stage(
        first_q, lambda to: qdup.at[pl.ds(to + FIRST_AT, FIRST_N)], fz_s, fz_r, fx_s, fx_r)
    send_rest, relay_rest, arrived_rest, finish_rest = two_stage(
        rest_q, lambda to: qdup.at[pl.ds(to + REST_AT, REST_N)], rz_s, rz_r, rx_s, rx_r)

    def unpack(buf, c, heads):
        for j, k in enumerate(heads):
            qg[k, pl.ds(c, GROUP, stride=QS), :] = buf[c, j].astype(f32)

    def take_first(c):
        unpack(first_q, c, FIRST_HEADS)

    def take_rest(c):
        unpack(rest_q, c, REST_HEADS)

    send_first()
    send_rest()
    take_first(ctx)
    take_rest(ctx)
    near_first = list(reversed(range(NZ - 1)))
    lag = 7
    for n in range(NZ - 1 + lag):
        if n < NZ - 1:
            relay_first(near_first[n])
        if n >= lag:
            relay_rest(near_first[n - lag])
    for i in near_first:
        take_first(source(i) * NX + x)
    for i in near_first:
        take_rest(source(i) * NX + x)
    for i in reversed(range(NZ)):
        for dx in range(1, NX):
            arrived_first(i, dx)
            take_first(source(i) * NX + at_x(-dx))
    for k in FIRST_HEADS:
        qb[k] = qg[k].astype(bf16)

    def wait_rest():
        for i in reversed(range(NZ)):
            for dx in range(1, NX):
                arrived_rest(i, dx)
                take_rest(source(i) * NX + at_x(-dx))
        for k in REST_HEADS:
            qb[k] = qg[k].astype(bf16)

    lane = lax.broadcasted_iota(jnp.int32, (CHUNK, HD), 1)
    line = lax.broadcasted_iota(jnp.int32, (CHUNK, HD), 0)
    diagonal = lane == line
    diagonal_high = lane == line + CHUNK
    low = lax.broadcasted_iota(jnp.int32, (1, HD), 1) < CHUNK

    def x_copies(k, dx):
        to = at_x(dx)
        where = peer(z, to)
        return (
            pltpu.make_async_remote_copy(
                osend.at[k, pl.ds(pl.multiple_of(to * CHUNK, CHUNK), CHUNK), :],
                xbuf.at[k, dx - 1], xs_s.at[k, dx - 1, 0], xs_r.at[k, dx - 1, 0],
                device_id=where, device_id_type=MESH),
            pltpu.make_async_remote_copy(
                ostat.at[k, to, pl.ds(0, 1), :], xstat.at[k, dx - 1, pl.ds(0, 1), :],
                xs_s.at[k, dx - 1, 1], xs_r.at[k, dx - 1, 1],
                device_id=where, device_id_type=MESH),
        )

    def z_copies(k, dz):
        where = peer(at_z(dz), x)
        return (
            pltpu.make_async_remote_copy(
                zsend.at[k], zbuf.at[k], zs_s.at[k, 0], zs_r.at[k, 0],
                device_id=where, device_id_type=MESH),
            pltpu.make_async_remote_copy(
                zsstat.at[k, pl.ds(0, 1), :], zstat.at[k, pl.ds(0, 1), :],
                zs_s.at[k, 1], zs_r.at[k, 1], device_id=where, device_id_type=MESH),
        )

    def join(parts):
        top = functools.reduce(jnp.maximum, [stat for stat, _ in parts])
        total = jnp.zeros_like(top)
        mixed = jnp.zeros((CHUNK, HD), f32)
        for stat, numerator in parts:
            factor = jnp.exp2(stat - top)
            total = total + pltpu.roll(factor, CHUNK, 1) * stat
            column = jnp.sum(
                jnp.where(diagonal, jnp.broadcast_to(factor, (CHUNK, HD)), 0.0),
                axis=1, keepdims=True)
            mixed = mixed + column * numerator.astype(f32)
        return jnp.where(low, top, total), mixed

    own_rows = pl.ds(pl.multiple_of(x * CHUNK, CHUNK), CHUNK)

    def join_x(k):
        parts = [(ostat[k, x, 0:1, :], osend[k, own_rows, :])]
        for dx in range(1, NX):
            for copy in x_copies(k, dx):
                copy.wait_recv()
            parts.append((xstat[k, dx - 1, 0:1, :], xbuf[k, dx - 1]))
        stat, mixed = join(parts)
        zsend[k] = mixed.astype(bf16)
        zsstat[k, 0:1, :] = stat
        if FAR_FIRST[k] != 0:
            for copy in z_copies(k, FAR_FIRST[k]):
                copy.start()

    scores = (s_even, s_odd)
    rounded = (p_even, p_odd)
    tile, block = 256, 16
    per = CHUNK // block
    b_lane = lax.broadcasted_iota(jnp.int32, (block, HD), 1)
    b_line = lax.broadcasted_iota(jnp.int32, (block, HD), 0)

    def score_tile(k, c):
        rows = slice(c * tile, (c + 1) * tile)
        query = jnp.concatenate([qb[k], hide[...]], axis=1)
        keys = jnp.concatenate([kbuf[k, rows, :], fbuf[rows, :]], axis=1)
        scores[k % 2][:, rows] = lax.dot_general(
            query, keys, (((1,), (1,)), ((), ())), preferred_element_type=f32)

    def soften(k, r, stat):
        rows = slice(r * block, (r + 1) * block)
        score = scores[k % 2][rows, :]
        top = jnp.max(score, axis=1, keepdims=True)
        weight = jnp.exp2((score - top) * SCALE2)
        total = jnp.sum(weight, axis=1, keepdims=True)
        rounded[k % 2][rows, :] = weight.astype(bf16)
        at = b_lane - b_line - (r % per) * block
        part = jnp.where(at == 0, top * SCALE2, 0.0) + jnp.where(at == CHUNK, total, 0.0)
        part = part[:8] + part[8:]
        stat = part if r % per == 0 else stat + part
        if r % per == per - 1:
            ostat[k, r // per, 0:1, :] = jnp.sum(stat, axis=0, keepdims=True)
        return stat

    def value_tile(k, c):
        rows = slice(c * tile, (c + 1) * tile)
        term = jnp.dot(rounded[k % 2][:, rows], vbuf[k, rows, :], preferred_element_type=f32)
        if c == 0:
            partial[k % 2] = term
        elif c < tiles - 1:
            partial[k % 2] = partial[k % 2] + term
        else:
            osend[k] = (partial[k % 2] + term).astype(bf16)

    tiles = span // tile
    for k in range(KVH):
        k_copies[k].wait()
        v_copies[k].wait()
    for i in range(KVH + 2):
        if i == FIRST_N:
            wait_rest()
        stat = None
        for r in range(ROWS // block):
            if 1 <= i <= KVH:
                stat = soften(i - 1, r, stat)
            if r % 2 == 0 and i < KVH:
                score_tile(i, r // 2)
            if r % 2 == 1 and i >= 2:
                value_tile(i - 2, r // 2)
        for k in SEND_AFTER.get(i, ()):
            for dx in (2, 1, 3):
                for copy in x_copies(k, dx):
                    copy.start()
        for k in JOIN_AFTER.get(i, ()):
            join_x(k)

    own = NZ - 1
    parts = [(zsstat[own, 0:1, :], zsend[own])]
    for k in range(NZ - 1):
        for copy in z_copies(k, FAR_FIRST[k]):
            copy.wait_recv()
        parts.append((zstat[k, 0:1, :], zbuf[k]))
    stat, mixed = join(parts)
    divisor = jnp.sum(
        jnp.where(diagonal_high, jnp.broadcast_to(stat, (CHUNK, HD)), 0.0), axis=1, keepdims=True)
    mixed = mixed / divisor
    abuf[ctx] = jnp.concatenate([mixed[:QS], mixed[QS:]], axis=1).astype(bf16)

    def chunk_copy(c, send, recv, where):
        return pltpu.make_async_remote_copy(
            abuf.at[c], abuf.at[c], send, recv, device_id=where, device_id_type=MESH)

    def a_z(i):
        return chunk_copy(ctx, az_s.at[i], az_r.at[i], peer(at_z(FAR_FIRST[i]), x))

    def a_x(i, dx):
        return chunk_copy(
            source(i) * NX + x, ax_s.at[i, dx - 1], ax_r.at[i, dx - 1], peer(z, at_x(dx)))

    def a_near(i, dx):
        return chunk_copy(
            z * NX + at_x(-dx), ax_s.at[i, dx - 1], ax_r.at[i, dx - 1],
            peer(at_z(FAR_FIRST[i]), x))

    def term(row):
        chunks = jnp.concatenate([abuf[row * NX + xx] for xx in range(NX)], axis=1)
        depth = NX * 2 * HD
        return jnp.dot(
            chunks, wbuf[pl.ds(pl.multiple_of(row * depth, depth), depth), :],
            preferred_element_type=f32)

    mine = NZ - 1
    for i in range(mine):
        a_z(i).start()
    for dx in (2, 1, 3):
        a_x(mine, dx).start()
    for dx in (1, 3, 2):
        a_x(mine, dx).wait_recv()
        for i in Z_NEAR:
            a_near(i, dx).start()
    for i in Z_FAR:
        a_z(i).wait_recv()
        for dx in (2, 1, 3):
            a_x(i, dx).start()
    w_copy.wait()
    projected = term(z)
    for i in Z_NEAR:
        a_z(i).wait_recv()
        for dx in (1, 3, 2):
            a_near(i, dx).wait_recv()
        projected = projected + term(source(i))
    for i in Z_FAR:
        for dx in (1, 3, 2):
            a_x(i, dx).wait_recv()
        projected = projected + term(source(i))

    def finish_a():
        for i in range(mine):
            a_z(i).wait_send()
            for dx in range(1, NX):
                (a_near if i in Z_NEAR else a_x)(i, dx).wait_send()
        for dx in range(1, NX):
            a_x(mine, dx).wait_send()

    ysend[...] = projected.astype(bf16)
    y_copy = pltpu.make_async_remote_copy(
        ysend, out_ref, y_s.at[0], y_r.at[0],
        device_id={"segment": after, "ctx": ctx}, device_id_type=MESH)
    y_copy.start()
    finish_first()
    finish_rest()
    finish_a()
    for k, dz in enumerate(FAR_FIRST):
        for dx in range(1, NX):
            for copy in x_copies(k, dx):
                copy.wait_send()
        if dz != 0:
            for copy in z_copies(k, dz):
                copy.wait_send()
    y_copy.wait()


def per_device(queries, cache, out_weight, offsets, starts):
    span = cache.shape[0]
    columns = out_weight.shape[1]
    bf16, f32 = jnp.bfloat16, jnp.float32
    dma = pltpu.SemaphoreType.DMA
    hop = [dma((NZ - 1,)), dma((NZ - 1,)), dma((NZ, NX - 1)), dma((NZ, NX - 1))]
    return pl.pallas_call(
        kernel,
        out_shape=jax.ShapeDtypeStruct((QS, columns), bf16),
        in_specs=[pl.BlockSpec(memory_space=pltpu.HBM)] * 5,
        out_specs=pl.BlockSpec(memory_space=pltpu.VMEM),
        scratch_shapes=[
            pltpu.SMEM((1,), jnp.int32),
            pltpu.SMEM((1,), jnp.int32),
            pltpu.VMEM((1, H * HD), bf16),
            pltpu.VMEM((H, HD), f32),
            pltpu.VMEM((REST_AT + REST_N + NZ - 1, GROUP, HD), bf16),
            pltpu.VMEM((QS, FIRST_N, GROUP, HD), bf16),
            pltpu.VMEM((QS, REST_N, GROUP, HD), bf16),
            pltpu.VMEM((KVH, ROWS, HD), f32),
            pltpu.VMEM((KVH, ROWS, HD), bf16),
            pltpu.VMEM((ROWS, HD), bf16),
            pltpu.VMEM((span, HD), bf16),
            pltpu.VMEM((KVH, span, HD), bf16),
            pltpu.VMEM((KVH, span, HD), bf16),
            pltpu.VMEM((H * HD, columns), bf16),
            pltpu.VMEM((ROWS, span), f32),
            pltpu.VMEM((ROWS, span), f32),
            pltpu.VMEM((ROWS, span), bf16),
            pltpu.VMEM((ROWS, span), bf16),
            pltpu.VMEM((2, ROWS, HD), f32),
            pltpu.VMEM((KVH, ROWS, HD), bf16),
            pltpu.VMEM((KVH, NX, 8, HD), f32),
            pltpu.VMEM((KVH, NX - 1, CHUNK, HD), bf16),
            pltpu.VMEM((KVH, NX - 1, 8, HD), f32),
            pltpu.VMEM((NZ, CHUNK, HD), bf16),
            pltpu.VMEM((NZ, 8, HD), f32),
            pltpu.VMEM((NZ, CHUNK, HD), bf16),
            pltpu.VMEM((NZ, 8, HD), f32),
            pltpu.VMEM((QS, QS, 2 * HD), bf16),
            pltpu.VMEM((QS, columns), bf16),
            dma((2,)), dma, dma((KVH,)), dma((KVH,)), dma,
            *hop, *hop,
            dma((KVH, NX - 1, 2)), dma((KVH, NX - 1, 2)),
            dma((NZ - 1, 2)), dma((NZ - 1, 2)),
            *hop,
            dma((1,)), dma((1,)),
        ],
        compiler_params=pltpu.CompilerParams(collective_id=0, has_side_effects=True, vmem_limit_bytes=VMEM_LIMIT),
        name="section_attention",
    )(offsets, starts, *[
        pltpu.with_memory_space_constraint(a, pltpu.HBM) for a in (queries, cache, out_weight)])


def solution(mesh):
    in_specs = (
        P(("segment", "ctx"), None),
        P(("segment", "ctx"), None),
        P("segment", "ctx"),
        P("segment"),
        P("segment"),
    )
    out_specs = P("segment", "ctx")
    return jax.shard_map(
        per_device, mesh=mesh, in_specs=in_specs, out_specs=out_specs, check_vma=False
    )
```
